32 devices in a mesh: head: 2 (over core), blk: 16 (over z, y, x).
Axes of the slice: x: 2, y: 2, z: 4, core: 2. Of those that a mesh axis runs over, the one named last changes fastest.
Arguments:
- inputs: bfloat16 [16, 1024, 768], P('blk', 'head'), may hold values from -6 to 6
- positions: int32 [16, 1024], P('blk', 'head'), may hold values from 0 to 15359, as said below
- w_query: bfloat16 [768, 768], P(('head', 'blk')), may hold values from -0.21875 to 0.21875
- w_key: bfloat16 [768, 768], P(('head', 'blk')), may hold values from -0.21875 to 0.21875
- w_value: bfloat16 [768, 768], P(('head', 'blk')), may hold values from -0.21875 to 0.21875
- w_out: bfloat16 [768, 768], P(('head', 'blk')), may hold values from -1.5 to 1.5
- w_up: bfloat16 [768, 3072], P(('head', 'blk')), may hold values from -0.21875 to 0.21875
- bias_up: bfloat16 [3072], P(('head', 'blk')), may hold values from -3 to 3
- w_down: bfloat16 [3072, 768], P(('head', 'blk')), may hold values from -0.109375 to 0.109375
- bias_down: bfloat16 [768], P(('head', 'blk')), may hold values from -3 to 3
- gain_mid: bfloat16 [768], P(('head', 'blk')), may hold values from 0.5 to 1.5
- shift_mid: bfloat16 [768], P(('head', 'blk')), may hold values from -3 to 3
- gain_out: bfloat16 [768], P(('head', 'blk')), may hold values from 0.5 to 1.5
- shift_out: bfloat16 [768], P(('head', 'blk')), may hold values from -3 to 3
- grad_out: bfloat16 [16, 1024, 768], P('blk', 'head'), may hold values from -6 to 6
Outputs:
- output: bfloat16 [16, 1024, 768], P('blk', 'head')
- grad_inputs: float32 [16, 1024, 768], P('blk', 'head')
- grad_w_query: float32 [768, 768], P(('head', 'blk'))
- grad_w_key: float32 [768, 768], P(('head', 'blk'))
- grad_w_value: float32 [768, 768], P(('head', 'blk'))
- grad_w_out: float32 [768, 768], P(('head', 'blk'))
- grad_w_up: float32 [768, 3072], P(('head', 'blk'))
- grad_bias_up: float32 [3072], P(('head', 'blk'))
- grad_w_down: float32 [3072, 768], P(('head', 'blk'))
- grad_bias_down: float32 [768], P(('head', 'blk'))
- grad_gain_mid: float32 [768], P(('head', 'blk'))
- grad_shift_mid: float32 [768], P(('head', 'blk'))
- grad_gain_out: float32 [768], P(('head', 'blk'))
- grad_shift_out: float32 [768], P(('head', 'blk'))
The draws below stay inside these ranges and needn't reach their ends.
Inputs may be any that keep to these rules, and one draw needn't show every extreme that they name: `positions`: positions count 0, 1, 2, ... from each document's first token. One document begins inside the first segment and is 15360 tokens long, so that it ends inside the last segment; shorter documents fill the stream before and after it.
All inputs are finite; a program needn't handle non-finite values.
Results may differ from the reference program's by a relative error of at most 0.017.
Values may be sent and summed in bfloat16 or wider, within the bound.
A program may use at most 192 MiB of HBM per device.

```python
import jax
import jax.numpy as jnp
from jax import lax

D = 768
HEADS = 12
HEAD_DIM = 64
FF = 3072
SUB = 512
SEG = 1024
SEGS = 16
TOKENS = 16384


def draw_positions(key, part):
    total_rows = SEGS * SEG
    first_key, second_key = jax.random.split(key)
    doc_begin = jax.random.randint(first_key, (), 1, SEG).astype(jnp.int32)
    finish = doc_begin + total_rows - SEG
    places = jnp.arange(total_rows, dtype=jnp.int32)
    coin_flips = jax.random.randint(second_key, (total_rows,), 0, 48) == 0
    outside = (places < doc_begin) | (places > finish)
    starts = (places == 0) | (places == doc_begin) | (places == finish) | coin_flips & outside
    last_start = lax.cummax(jnp.where(starts, places, 0), axis=0)
    return (places - last_start).reshape(SEGS, SEG).astype(jnp.int32)


def block_levels(key, extent, cuts, low, high):
    def one(dim, shards_of):
        steps = jax.random.uniform(jax.random.fold_in(jax.random.fold_in(key, 6), dim), (shards_of,), jnp.float32, low / len(cuts), high / len(cuts))
        return jnp.repeat(jnp.exp(steps), extent[dim] // shards_of).reshape((-1,) + (1,) * (len(extent) - dim - 1))

    level = one(*cuts[0])
    for cut in cuts[1:]:
        level = level * one(*cut)
    return level


def noise(key, extent, scale, reach, cuts=(), kind=jnp.bfloat16):
    array = jax.random.normal(key, extent, jnp.float32) * scale
    if len(cuts) > 0:
        array = block_levels(key, extent, cuts, -0.22, 0.18) * array
    return jnp.clip(array, min=-reach, max=reach).astype(kind)


def setup_inputs(seed: int = 0) -> dict:
    streams_of = jax.random.split(jax.random.key(seed), 16)
    inputs = noise(streams_of[0], (SEGS, SEG, D), 1.0, 6.0, ((0, 16), (1, 2)))
    positions = draw_positions(jax.random.fold_in(streams_of[15], 71), 0)
    w_query = noise(streams_of[2], (D, D), D ** -0.5, 0.21875, ((0, 32),))
    w_key = noise(streams_of[3], (D, D), D ** -0.5, 0.21875, ((0, 32),))
    w_value = noise(streams_of[4], (D, D), D ** -0.5, 0.21875, ((0, 32),))
    w_out = noise(streams_of[5], (D, D), (HEAD_DIM // 4) ** -0.5, 1.5, ((0, 32),))
    w_up = noise(streams_of[6], (D, FF), D ** -0.5, 0.21875, ((0, 32),))
    bias_up = noise(streams_of[7], (FF,), 0.5, 3.0, ((0, 32),))
    w_down = noise(streams_of[8], (FF, D), FF ** -0.5, 0.109375, ((0, 32),))
    bias_down = noise(streams_of[9], (D,), 0.5, 3.0, ((0, 32),))
    gain_mid = jnp.clip(1.0 + 0.1 * jax.random.normal(streams_of[10], (D,), jnp.float32), 0.5, 1.5).astype(jnp.bfloat16)
    shift_mid = noise(streams_of[11], (D,), 0.5, 3.0, ((0, 32),))
    gain_out = jnp.clip(1.0 + 0.1 * jax.random.normal(streams_of[12], (D,), jnp.float32), 0.5, 1.5).astype(jnp.bfloat16)
    shift_out = noise(streams_of[13], (D,), 0.5, 3.0, ((0, 32),))
    grad_out = noise(streams_of[14], (SEGS, SEG, D), 1.0, 6.0, ((0, 16), (1, 2)))
    return {"inputs": inputs, "positions": positions, "w_query": w_query, "w_key": w_key, "w_value": w_value, "w_out": w_out, "w_up": w_up, "bias_up": bias_up, "w_down": w_down, "bias_down": bias_down, "gain_mid": gain_mid, "shift_mid": shift_mid, "gain_out": gain_out, "shift_out": shift_out, "grad_out": grad_out}


eps = 1e-05
half_pi = 1.5707963267948966
highest = lax.Precision.HIGHEST

@jax.custom_vjp
def low(v):
    return lax.optimization_barrier(v.astype(jnp.bfloat16)).astype(jnp.float32)

@jax.custom_vjp
def low_back(v):
    return v

def low_keep(v):
    return (low(v), None)

def low_pass(kept, grad):
    return (grad,)

def back_keep(v):
    return (v, None)

def back_low(kept, grad):
    return (low(grad),)
low.defvjp(low_keep, low_pass)
low_back.defvjp(back_keep, back_low)

def block_tail(block_positions):
    width_now = block_positions.shape[-1]
    places = jnp.arange(width_now, dtype=jnp.int32)
    last_position = block_positions[..., width_now - 1:]
    tail_mask = (width_now - 1 - places <= last_position).astype(jnp.float32)
    keeping = (last_position >= width_now).astype(jnp.float32)
    return (tail_mask, keeping)

def block_masks(block_positions):
    width_now = block_positions.shape[-1]
    places = jnp.arange(width_now, dtype=jnp.int32)
    causal = ((places[None, :] <= places[:, None]) & (places[:, None] - places[None, :] <= block_positions[:, None])).astype(jnp.float32)
    use_mask = (block_positions > places).astype(jnp.float32)
    tail_mask, keeping = block_tail(block_positions)
    return (causal, use_mask, tail_mask, keeping)

def layer_norm(values, gain_factor, shift_term):
    centered = values - lax.optimization_barrier(jnp.mean(values, axis=-1, keepdims=True))
    return centered * lax.rsqrt(lax.optimization_barrier(jnp.mean(centered * centered, axis=-1, keepdims=True)) + eps) * gain_factor + shift_term

def forward(floats, positions):
    inputs, w_query, w_key, w_value, w_out, w_up, bias_up, w_down, bias_down, gain_mid, shift_mid, gain_out, shift_out = floats
    blocks = TOKENS // SUB
    rows_all = inputs.reshape(blocks, SUB, D)
    position_blocks = positions.reshape(blocks, SUB)

    def block_step(carried, block_data):
        row_block, block_positions = block_data
        causal, use_mask, tail_mask, keeping = block_masks(block_positions)
        angles = block_positions.astype(jnp.float32) * (half_pi / TOKENS)
        cosine = jnp.cos(angles)[:, None, None]
        sine_wave = jnp.sin(angles)[:, None, None]

        def project(weight):
            return low(low_back(jnp.dot(row_block, weight, precision=highest))).reshape(SUB, HEADS, HEAD_DIM)

        def features(raw_rows):
            soft_part = jax.nn.softplus(raw_rows)
            return low(jnp.concatenate([soft_part * cosine, soft_part * sine_wave], axis=-1))
        query_features = features(project(w_query))
        key_features = features(project(w_key))
        values = project(w_value)
        state_in, total_in = carried
        scores = jnp.einsum('ihf,jhf->hij', query_features, key_features, precision=highest) * causal[None]
        weights = low(low_back(scores))
        numerator = jnp.einsum('hij,jhd->ihd', weights, values, precision=highest)
        numerator = numerator + use_mask[:, None, None] * jnp.einsum('ihf,hfd->ihd', query_features, state_in, precision=highest)
        numerator = low_back(numerator)
        denominator = lax.optimization_barrier(jnp.sum(weights, axis=2)).T + use_mask[:, None] * jnp.einsum('ihf,hf->ih', query_features, total_in, precision=highest)
        mixed_rows = low(low_back(numerator / denominator[:, :, None])).reshape(SUB, D)
        weighted = key_features * tail_mask[:, None, None]
        new_state = keeping * state_in + jnp.einsum('jhf,jhd->hfd', weighted, values, precision=highest)
        new_total = keeping * total_in + lax.optimization_barrier(jnp.sum(weighted, axis=0))
        middle = row_block + low_back(jnp.dot(mixed_rows, w_out, precision=highest))
        mid_rows = layer_norm(middle, gain_mid, shift_mid)
        up_rows = low_back(jnp.dot(low(mid_rows), w_up, precision=highest) + bias_up)
        active = low(jax.nn.gelu(up_rows))
        after_ffn = mid_rows + low_back(jnp.dot(active, w_down, precision=highest) + bias_down)
        return ((new_state, new_total), layer_norm(after_ffn, gain_out, shift_out))
    start_carry = (jnp.zeros((HEADS, 2 * HEAD_DIM, HEAD_DIM), jnp.float32), jnp.zeros((HEADS, 2 * HEAD_DIM), jnp.float32))
    final_carry, results = lax.scan(jax.checkpoint(block_step), start_carry, (rows_all, position_blocks))
    return results.reshape(SEGS, SEG, D)

def reference(inputs, positions, w_query, w_key, w_value, w_out, w_up, bias_up, w_down, bias_down, gain_mid, shift_mid, gain_out, shift_out, grad_out):
    floats = (inputs.astype(jnp.float32), w_query.astype(jnp.float32), w_key.astype(jnp.float32), w_value.astype(jnp.float32), w_out.astype(jnp.float32), w_up.astype(jnp.float32), bias_up.astype(jnp.float32), w_down.astype(jnp.float32), bias_down.astype(jnp.float32), gain_mid.astype(jnp.float32), shift_mid.astype(jnp.float32), gain_out.astype(jnp.float32), shift_out.astype(jnp.float32))

    def forward_floats(*arguments):
        return forward(arguments, positions)
    output, pullback = jax.vjp(forward_floats, *floats)
    gradients = pullback(grad_out.astype(jnp.float32))
    return (output.astype(jnp.bfloat16), gradients[0], gradients[1], gradients[2], gradients[3], gradients[4], gradients[5], gradients[6], gradients[7], gradients[8], gradients[9], gradients[10], gradients[11], gradients[12])
```

```python
import functools

import jax
import jax.numpy as jnp
from jax import lax
from jax.experimental import pallas as pl
from jax.experimental.pallas import tpu as pltpu
from jax.sharding import PartitionSpec as P

HEADS = 12
HEAD_DIM = 64
SUB = 512
PAIRS = HEADS // 2

eps = 1e-05
half_pi = 1.5707963267948966
f32 = jnp.float32
bf16 = jnp.bfloat16
MESH = pl.DeviceIdType.MESH
VMEM_BYTES = 58 << 20


class Grid:
    def __init__(self, chips):
        if chips == 16:
            self.inner, self.a, self.n, self.strides = 1, 4, 2, (1, 2)
            self.line = ((2, 1), (2, 2), (4, 4))
        elif chips == 128:
            self.inner, self.a, self.n, self.strides = 8, 1, 4, (1, 4)
            self.line = ((8, 1), (4, 8), (4, 32))
        else:
            raise ValueError(chips)
        self.groups = 16

    def lanes(self):
        return [
            [group * self.inner + lane for lane in range(self.inner)]
            for group in range(self.groups)
        ]


class Place:
    def __init__(self, grid):
        self.grid = grid
        self.core = lax.axis_index("head")
        self.blk = lax.axis_index("blk")
        group = self.blk // grid.inner
        self.lane = self.blk - group * grid.inner
        n, (near, far) = grid.n, grid.strides
        first = group // near % n
        second = group // far % n
        self.a = group // (n * n)
        flip = self.core == 0
        self.b = jnp.where(flip, first, second)
        self.c = jnp.where(flip, second, first)
        self.step_b = jnp.where(flip, near, far)
        self.step_c = jnp.where(flip, far, near)
        self.me = group

    def shard(self, a, b, c):
        return a * (self.grid.n * self.grid.n) + b * self.step_b + c * self.step_c

    def device(self, shard):
        return (self.core, shard * self.grid.inner + self.lane)

    def turn_a(self, d):
        return (self.a + d) % self.grid.a

    def turn_b(self, d):
        return (self.b + d) % self.grid.n

    def turn_c(self, d):
        return (self.c + d) % self.grid.n

    def peers_a(self):
        return [
            self.device(self.shard(self.turn_a(d), self.b, self.c))
            for d in range(1, self.grid.a)
        ]

    def peers_b(self):
        return [
            self.device(self.shard(self.a, self.turn_b(d), self.c))
            for d in range(1, self.grid.n)
        ]

    def peers_c(self):
        return [
            self.device(self.shard(self.a, self.b, self.turn_c(d)))
            for d in range(1, self.grid.n)
        ]

    def partner(self):
        return (1 - self.core, self.blk)


def greet(peers):
    barrier = pltpu.get_barrier_semaphore()
    for peer in peers:
        pl.semaphore_signal(barrier, inc=1, device_id=peer, device_id_type=MESH)
    pl.semaphore_wait(barrier, len(peers))


def send(src, dst, sent, got, device):
    pltpu.make_async_remote_copy(
        src_ref=src,
        dst_ref=dst,
        send_sem=sent,
        recv_sem=got,
        device_id=device,
        device_id_type=MESH,
    ).start()


def await_bytes(ref, sem):
    pltpu.make_async_copy(ref, ref, sem).wait()


def params(number=None):
    if number is None:
        return pltpu.CompilerParams(vmem_limit_bytes=VMEM_BYTES)
    return pltpu.CompilerParams(
        collective_id=number, has_side_effects=True, vmem_limit_bytes=VMEM_BYTES
    )


HBM_SPEC = pl.BlockSpec(memory_space=pltpu.HBM)
VMEM_SPEC = pl.BlockSpec(memory_space=pltpu.VMEM)


def vector_sum(place, vec, total, slots, sent, got):
    total[...] = vec[...]
    steps = (
        [place.partner()],
        place.peers_b(),
        place.peers_c(),
        place.peers_a(),
    )
    base = 0
    for number, peers in enumerate(steps):
        if not peers:
            continue
        for d, peer in enumerate(peers):
            send(total, slots.at[base + d], sent.at[number], got.at[number], peer)
        view = slots.at[pl.ds(base, len(peers))]
        await_bytes(view, got.at[number])
        await_bytes(view, sent.at[number])
        value = total[...]
        for d in range(len(peers)):
            value = value + slots[base + d]
        total[...] = value
        base += len(peers)


def gather_kernel(grid, units, count, *refs):
    shards, vec = refs[:count], refs[count]
    full, total = refs[count + 1 : 2 * count + 1], refs[2 * count + 1]
    slots, own, out_sem, got_a, got_b, got_bz, got_c, pair_out, got_p, vs, vg = refs[2 * count + 2 :]
    place = Place(grid)
    na, n = grid.a, grid.n
    greet(place.peers_a() + place.peers_b() + place.peers_c() + [place.partner()])
    core, partner = place.core, place.partner()

    def piece(u):
        w, r0, r, c0, c = units[u]
        return shards[w].at[pl.ds(r0, r), pl.ds(c0, c)]

    def slot(u, s):
        w, r0, r, c0, c = units[u]
        return full[w].at[core, s, pl.ds(r0, r), pl.ds(c0, c)]

    def many(u, k):
        w, r0, r, c0, c = units[u]
        return full[w].at[core, pl.ds(0, k), pl.ds(r0, r), pl.ds(c0, c)]

    def pass_on(u, s, peers, got):
        for peer in peers:
            send(slot(u, s), slot(u, s), out_sem.at[u], got.at[u], peer)

    def start(u):
        pltpu.make_async_copy(piece(u), slot(u, place.me), own.at[u]).start()
        for peers, got in (
            (place.peers_a(), got_a),
            (place.peers_b(), got_b),
            (place.peers_c(), got_c),
        ):
            for peer in peers:
                send(piece(u), slot(u, place.me), out_sem.at[u], got.at[u], peer)
        send(piece(u), slot(u, place.me), pair_out.at[u], got_p.at[u], partner)

    def after_a(u):
        if na > 1:
            await_bytes(many(u, na - 1), got_a.at[u])
        for d in range(1, na):
            pass_on(u, place.shard(place.turn_a(d), place.b, place.c), place.peers_b(), got_bz)
        await_bytes(many(u, n - 1), got_b.at[u])
        for d in range(1, n):
            pass_on(u, place.shard(place.a, place.turn_b(d), place.c), place.peers_c(), got_c)
        for d in range(1, na):
            pass_on(u, place.shard(place.turn_a(d), place.b, place.c), place.peers_c(), got_c)

    def after_b(u):
        if na > 1:
            await_bytes(many(u, (na - 1) * (n - 1)), got_bz.at[u])
        for d in range(na):
            for e in range(n):
                s = place.shard(place.turn_a(d), place.turn_b(e), place.c)
                if d > 0 and e > 0:
                    pass_on(u, s, place.peers_c(), got_c)
                if d > 0 or e > 0:
                    send(slot(u, s), slot(u, s), pair_out.at[u], got_p.at[u], partner)

    def after_c(u):
        await_bytes(many(u, na * n * (n - 1)), got_c.at[u])
        for d in range(na):
            for e in range(n):
                for f in range(1, n):
                    s = place.shard(place.turn_a(d), place.turn_b(e), place.turn_c(f))
                    send(slot(u, s), slot(u, s), pair_out.at[u], got_p.at[u], partner)

    ahead = 4
    size = len(units)
    for u in range(min(ahead, size)):
        start(u)
    for step in range(size + 2):
        if step < size:
            after_a(step)
        if step + ahead < size:
            start(step + ahead)
        if 0 <= step - 1 < size:
            after_b(step - 1)
        if 0 <= step - 2 < size:
            after_c(step - 2)
    vector_sum(place, vec, total, slots, vs, vg)
    sends = (na - 1) + 2 * (n - 1) + (na - 1) * (n - 1) + (n - 1) * (na * n - 1)
    for u in range(size):
        await_bytes(many(u, 1), own.at[u])
        await_bytes(many(u, 16), got_p.at[u])
        await_bytes(many(u, 16), pair_out.at[u])
        left = sends
        while left > 0:
            await_bytes(many(u, min(left, 16)), out_sem.at[u])
            left -= 16


def split_units(shapes):
    units = []
    for w, (r, c) in enumerate(shapes):
        if c > 1024:
            for part in range(2):
                units.append((w, 0, r, part * c // 2, c // 2))
        elif r > 48:
            for part in range(2):
                units.append((w, part * r // 2, r // 2, 0, c))
        else:
            units.append((w, 0, r, 0, c))
    return tuple(units)


def gather_weights(grid, weights, vec):
    shapes = [w.shape for w in weights]
    units = split_units(shapes)
    size = len(units)
    dma = pltpu.SemaphoreType.DMA((size,))
    peers = 1 + 2 * (grid.n - 1) + (grid.a - 1)
    out = pl.pallas_call(
        functools.partial(gather_kernel, grid, units, len(weights)),
        out_shape=tuple(jax.ShapeDtypeStruct((2, 16) + s, bf16) for s in shapes)
        + (jax.ShapeDtypeStruct(vec.shape, f32),),
        in_specs=[HBM_SPEC] * len(weights) + [VMEM_SPEC],
        out_specs=(HBM_SPEC,) * len(weights) + (VMEM_SPEC,),
        scratch_shapes=[pltpu.VMEM((peers,) + vec.shape, f32)]
        + [dma] * 8
        + [pltpu.SemaphoreType.DMA((4,))] * 2,
        compiler_params=params(1),
        name="gather_weights",
    )(*weights, vec)
    return [o.reshape(32 * s[0], s[1]) for o, s in zip(out, shapes)], out[-1]


def scatter_kernel(grid, units, count, *refs):
    grads, vec = refs[:count], refs[count]
    out, total = refs[count + 1 : 2 * count + 1], refs[2 * count + 1]
    rest = refs[2 * count + 2 :]
    size = len(units)
    acc, in_p, in_c, in_b, in_a, res = (rest[k * size : (k + 1) * size] for k in range(6))
    (slots, own, out_p, got_p, out_c, got_c, out_b, got_b, out_a, got_a, done, vs, vg) = rest[
        6 * size :
    ]
    place = Place(grid)
    na, n = grid.a, grid.n
    core = place.core
    greet(place.peers_a() + place.peers_b() + place.peers_c() + [place.partner()])

    def grad(u, side):
        w, r0, r, c0, c = units[u]
        return grads[w].at[side, :, pl.ds(r0, r), pl.ds(c0, c)]

    def add(u, s, value):
        acc[u][s] = (acc[u][s].astype(f32) + value.astype(f32)).astype(bf16)

    def start(u):
        send(grad(u, 1 - core), in_p[u], out_p.at[u], got_p.at[u], place.partner())
        pltpu.make_async_copy(grad(u, core), acc[u], own.at[u]).start()

    def after_p(u):
        await_bytes(in_p[u], got_p.at[u])
        await_bytes(acc[u], own.at[u])
        for f in list(range(1, n)) + [0]:

            def step(i, carry):
                s = place.shard(i // n, i % n, place.turn_c(f))
                add(u, s, in_p[u][s])
                if f > 0:
                    send(
                        acc[u].at[s],
                        in_c[u].at[f - 1, i],
                        out_c.at[u],
                        got_c.at[u],
                        place.peers_c()[f - 1],
                    )
                return carry

            lax.fori_loop(0, na * n, step, 0)

    def after_c(u):
        await_bytes(in_c[u], got_c.at[u])
        for e in list(range(1, n)) + [0]:

            def step(i, carry):
                s = place.shard(i, place.turn_b(e), place.c)
                j = i * n + place.turn_b(e)
                value = in_c[u][0, j].astype(f32)
                for f in range(1, n - 1):
                    value = value + in_c[u][f, j].astype(f32)
                add(u, s, value)
                if e > 0:
                    send(
                        acc[u].at[s],
                        in_b[u].at[e - 1, i],
                        out_b.at[u],
                        got_b.at[u],
                        place.peers_b()[e - 1],
                    )
                return carry

            lax.fori_loop(0, na, step, 0)

    def after_b(u):
        await_bytes(in_b[u], got_b.at[u])
        for d in list(range(1, na)) + [0]:
            i = place.turn_a(d)
            s = place.shard(i, place.b, place.c)
            value = in_b[u][0, i].astype(f32)
            for e in range(1, n - 1):
                value = value + in_b[u][e, i].astype(f32)
            add(u, s, value)
            if d > 0:
                send(acc[u].at[s], in_a[u].at[d - 1], out_a.at[u], got_a.at[u], place.device(s))

    def after_a(u):
        w, r0, r, c0, c = units[u]
        value = acc[u][place.me].astype(f32)
        if na > 1:
            await_bytes(in_a[u], got_a.at[u])
            for d in range(na - 1):
                value = value + in_a[u][d].astype(f32)
        res[u][...] = value
        pltpu.make_async_copy(res[u], out[w].at[pl.ds(r0, r), pl.ds(c0, c)], done.at[u]).start()

    for u in range(size):
        start(u)
    for step in range(size + 3):
        if step < size:
            after_p(step)
        if 0 <= step - 1 < size:
            after_c(step - 1)
        if 0 <= step - 2 < size:
            after_b(step - 2)
        if 0 <= step - 3 < size:
            after_a(step - 3)
    vector_sum(place, vec, total, slots, vs, vg)
    for u in range(size):
        await_bytes(in_p[u], out_p.at[u])
        await_bytes(in_c[u], out_c.at[u])
        await_bytes(in_b[u], out_b.at[u])
        if na > 1:
            await_bytes(in_a[u], out_a.at[u])
        await_bytes(res[u], done.at[u])


def scatter_grads(grid, grads, vec, shapes):
    units = split_units(shapes)
    size = len(units)
    na, n = grid.a, grid.n
    dma = pltpu.SemaphoreType.DMA((size,))

    def room(*lead):
        return [pltpu.VMEM(lead + (u[2], u[4]), bf16) for u in units]

    peers = 1 + 2 * (n - 1) + (na - 1)
    out = pl.pallas_call(
        functools.partial(scatter_kernel, grid, units, len(grads)),
        out_shape=tuple(jax.ShapeDtypeStruct(s, f32) for s in shapes)
        + (jax.ShapeDtypeStruct(vec.shape, f32),),
        in_specs=[HBM_SPEC] * len(grads) + [VMEM_SPEC],
        out_specs=(HBM_SPEC,) * len(grads) + (VMEM_SPEC,),
        scratch_shapes=room(16)
        + room(16)
        + room(n - 1, na * n)
        + room(n - 1, na)
        + room(max(na - 1, 1))
        + [pltpu.VMEM((u[2], u[4]), f32) for u in units]
        + [pltpu.VMEM((peers,) + vec.shape, f32)]
        + [dma] * 10
        + [pltpu.SemaphoreType.DMA((4,))] * 2,
        compiler_params=params(2),
        name="scatter_grads",
    )(*[g.reshape((2, 16) + s) for g, s in zip(grads, shapes)], vec)
    return out[:-1], out[-1]


def fold(state, total, state_next, total_next):
    keep = total_next[2:3, :]
    row = lax.broadcasted_iota(jnp.int32, total_next.shape, 0)
    return (
        keep[:, :128] * state + state_next,
        keep * total + jnp.where(row == 2, 0.0, total_next),
    )


def neutral(state_shape, total_shape):
    row = lax.broadcasted_iota(jnp.int32, total_shape, 0)
    return jnp.zeros(state_shape, f32), jnp.where(row == 2, 1.0, 0.0).astype(f32)


def state_kernel(grid, backward, *refs):
    state, total, entering, entering_total = refs[:4]
    own_s, pair_s, pair_t, fin_s, fin_t = refs[4:9]
    lines = len(grid.line)
    slot_s, slot_t, exc_s, exc_t = (refs[9 + k * lines : 9 + (k + 1) * lines] for k in range(4))
    so, sg, to, tg = refs[9 + 4 * lines :]
    core, blk = lax.axis_index("head"), lax.axis_index("blk")
    partner = (1 - core, blk)
    places = [blk // stride % size for size, stride in grid.line]

    def line_peers(d):
        size, stride = grid.line[d]
        at = places[d]
        return [(core, blk + ((at + k) % size - at) * stride) for k in range(1, size)]

    greet([partner] + [p for d in range(lines) for p in line_peers(d)])
    half = pl.ds(core * 3, 3)
    wide = pl.ds(pl.multiple_of(core * 384, 384), 384)
    own_s[...] = state[...].astype(bf16)
    send(own_s, pair_s, so.at[0], sg.at[0], partner)
    send(total, pair_t, to.at[0], tg.at[0], partner)
    await_bytes(pair_s, sg.at[0])
    await_bytes(pair_t, tg.at[0])
    first = (core == 1) if backward else (core == 0)
    mine = state[half], total[:, wide]
    theirs = pair_s[half].astype(f32), pair_t[:, wide]
    ahead = [jnp.where(first, m, t) for m, t in zip(mine, theirs)]
    behind = [jnp.where(first, t, m) for m, t in zip(mine, theirs)]
    run_s, run_t = fold(*ahead, *behind)
    for d in range(lines):
        size, stride = grid.line[d]
        at = places[d]
        slot_s[d][at] = run_s.astype(bf16)
        slot_t[d][at] = run_t
        for peer in line_peers(d):
            send(slot_s[d].at[at], slot_s[d].at[at], so.at[d + 1], sg.at[d + 1], peer)
            send(slot_t[d].at[at], slot_t[d].at[at], to.at[d + 1], tg.at[d + 1], peer)
        await_bytes(slot_s[d].at[pl.ds(0, size - 1)], sg.at[d + 1])
        await_bytes(slot_t[d].at[pl.ds(0, size - 1)], tg.at[d + 1])
        run_s, run_t = neutral(run_s.shape, run_t.shape)
        part_s, part_t = run_s, run_t
        for j in range(size - 1, -1, -1) if backward else range(size):
            next_s, next_t = slot_s[d][j].astype(f32), slot_t[d][j]
            before = (j > at) if backward else (j < at)
            added_s, added_t = fold(part_s, part_t, next_s, next_t)
            part_s = jnp.where(before, added_s, part_s)
            part_t = jnp.where(before, added_t, part_t)
            if d < lines - 1:
                run_s, run_t = fold(run_s, run_t, next_s, next_t)
        exc_s[d][...] = part_s
        exc_t[d][...] = part_t
    part_s, part_t = exc_s[lines - 1][...], exc_t[lines - 1][...]
    for d in range(lines - 2, -1, -1):
        part_s, part_t = fold(part_s, part_t, exc_s[d][...], exc_t[d][...])
    fin_s[half] = part_s.astype(bf16)
    fin_t[core] = part_t
    send(fin_s.at[half], fin_s.at[half], so.at[lines + 1], sg.at[lines + 1], partner)
    send(fin_t.at[core], fin_t.at[core], to.at[lines + 1], tg.at[lines + 1], partner)
    await_bytes(fin_s.at[half], sg.at[lines + 1])
    await_bytes(fin_t.at[core], tg.at[lines + 1])
    chip_s = fin_s[...].astype(f32)
    chip_t = jnp.concatenate([fin_t[0], fin_t[1]], axis=1)
    after_s, after_t = fold(chip_s, chip_t, pair_s[...].astype(f32), pair_t[...])
    entering[...] = jnp.where(first, chip_s, after_s).astype(bf16)
    entering_total[...] = jnp.where(first, chip_t, after_t)
    await_bytes(pair_s, so.at[0])
    await_bytes(pair_t, to.at[0])
    for d in range(lines):
        size, stride = grid.line[d]
        await_bytes(slot_s[d].at[pl.ds(0, size - 1)], so.at[d + 1])
        await_bytes(slot_t[d].at[pl.ds(0, size - 1)], to.at[d + 1])
    await_bytes(fin_s.at[half], so.at[lines + 1])
    await_bytes(fin_t.at[core], to.at[lines + 1])


def exchange_states(grid, state, total, backward):
    lines = grid.line
    sem = pltpu.SemaphoreType.DMA((len(lines) + 2,))
    return pl.pallas_call(
        functools.partial(state_kernel, grid, backward),
        out_shape=(
            jax.ShapeDtypeStruct((PAIRS, 128, 128), bf16),
            jax.ShapeDtypeStruct((8, 768), f32),
        ),
        in_specs=[VMEM_SPEC] * 2,
        out_specs=(VMEM_SPEC,) * 2,
        scratch_shapes=[
            pltpu.VMEM((PAIRS, 128, 128), bf16),
            pltpu.VMEM((PAIRS, 128, 128), bf16),
            pltpu.VMEM((8, 768), f32),
            pltpu.VMEM((PAIRS, 128, 128), bf16),
            pltpu.VMEM((2, 8, 384), f32),
        ]
        + [pltpu.VMEM((size, 3, 128, 128), bf16) for size, _ in lines]
        + [pltpu.VMEM((size, 8, 384), f32) for size, _ in lines]
        + [pltpu.VMEM((3, 128, 128), f32) for _ in lines]
        + [pltpu.VMEM((8, 384), f32) for _ in lines]
        + [sem] * 4,
        compiler_params=params(4 if backward else 3),
        name="exchange_states",
    )(state, total)


def dot(a, b, contract=((1,), (0,))):
    return lax.dot_general(a, b, (contract, ((), ())), preferred_element_type=f32)


def tall(row):
    return jnp.transpose(jnp.broadcast_to(row, (128, row.shape[1])))


def lane_side(shape):
    return lax.broadcasted_iota(jnp.int32, shape, 1) < HEAD_DIM


def ones_by_head():
    rows = lax.broadcasted_iota(jnp.int32, (128, 128), 0) < HEAD_DIM
    return jnp.where(rows == lane_side((128, 128)), 1.0, 0.0).astype(bf16)


def widen(compact):
    side = lane_side((64, 128))
    zero = jnp.zeros((64, 128), compact.dtype)
    parts = []
    for k in range(2):
        piece = compact[64 * k : 64 * k + 64]
        parts += [jnp.where(side, piece, zero), jnp.where(side, zero, piece)]
    return jnp.concatenate(parts, axis=0)


def compact_of(full):
    return jnp.where(lane_side((64, 128)), full[:64], full[64:])


def sum_by_head(value):
    high = value.astype(bf16)
    low = (value - high.astype(f32)).astype(bf16)
    ones = ones_by_head()
    return dot(jnp.concatenate([high, low], axis=1), jnp.concatenate([ones, ones], axis=0))


def position_terms(row, reach):
    place = row.astype(f32)
    angle = place * (half_pi / reach)
    cosine, sine = tall(jnp.cos(angle)), tall(jnp.sin(angle))
    column = tall(place)
    index = lax.broadcasted_iota(jnp.int32, column.shape, 0).astype(f32)
    use = (column > index).astype(f32)
    last = column[SUB - 1 : SUB, :]
    tail = ((SUB - 1) - index <= last).astype(f32)
    keep = (last >= SUB).astype(f32)
    return cosine, sine, use, tail, keep


def projections_kernel(reach, tok, wq, wk, wv, pos, q_out, k_out, v_out, sq_out, sk_out, state, total):
    rows = tok[...]
    cosine, sine, use, tail, keep = position_terms(pos[...], reach)
    for weight, raw, soft in ((wq, q_out, sq_out), (wk, k_out, sk_out), (wv, v_out, None)):
        for part in range(3):
            cols = slice(256 * part, 256 * part + 256)
            value = dot(rows, weight[:, cols]).astype(bf16)
            raw[:, cols] = value
            if soft is not None:
                wide = value.astype(f32)
                soft[:, cols] = jnp.maximum(wide, 0.0) + jnp.log1p(jnp.exp(-jnp.abs(wide)))
    for p in range(PAIRS):
        cols = slice(128 * p, 128 * p + 128)
        soft = sk_out[:, cols] * tail
        value = v_out[:, cols]
        for k, wave in enumerate((cosine, sine)):
            feature = (soft * wave).astype(bf16)
            state[p, 64 * k : 64 * k + 64, :] = compact_of(dot(feature, value, ((0,), (0,))))
            total[k : k + 1, cols] = jnp.sum(feature.astype(f32), axis=0, keepdims=True)
        total[2:3, cols] = keep
        total[3:8, cols] = jnp.zeros((5, 128), f32)


def mask_of(row, reach, flipped):
    place = row.astype(f32)
    angle = place * (half_pi / reach)
    cos_row, sin_row = jnp.cos(angle), jnp.sin(angle)
    across = lambda r: jnp.broadcast_to(r, (SUB, SUB))
    down = lambda r: jnp.transpose(across(r))
    i = lax.broadcasted_iota(jnp.int32, (SUB, SUB), 1 if flipped else 0)
    j = lax.broadcasted_iota(jnp.int32, (SUB, SUB), 0 if flipped else 1)
    spot = across(place) if flipped else down(place)
    seen = (j <= i) & ((i - j).astype(f32) <= spot)
    wave = down(cos_row) * across(cos_row) + down(sin_row) * across(sin_row)
    return jnp.where(seen, wave, 0.0)


def attend_kernel(reach, pos, sq, sk, v, entering, entering_total, mixed, inverse, mask):
    mask[...] = mask_of(pos[...], reach, False)
    cosine, sine, use, tail, keep = position_terms(pos[...], reach)
    ones = jnp.ones((SUB, 128), bf16)
    side = lane_side((SUB, 128))

    def one(p, carry):
        cols = pl.ds(pl.multiple_of(128 * p, 128), 128)
        soft = sq[:, cols]
        key = sk[:, cols].astype(bf16)
        values = jnp.concatenate([v[:, cols], ones], axis=1)
        qc, qs = soft * (cosine * use), soft * (sine * use)
        wide = widen(entering[p])
        num = dot(jnp.concatenate([qc, qs], axis=1).astype(bf16), wide)
        den = sum_by_head(qc * entering_total[0:1, cols] + qs * entering_total[1:2, cols])
        query = soft.astype(bf16)
        zero = jnp.zeros_like(query)
        outs = []
        for pick in (jnp.where(side, query, zero), jnp.where(side, zero, query)):
            top = (dot(pick[:256], key[:256], ((1,), (1,))) * mask[:256, :256]).astype(bf16)
            low = (dot(pick[256:], key, ((1,), (1,))) * mask[256:, :]).astype(bf16)
            outs.append(jnp.concatenate([dot(top, values[:256]), dot(low, values)], axis=0))
        num = num + jnp.where(side, outs[0][:, :128], outs[1][:, :128])
        den = den + jnp.where(side, outs[0][:, 128:], outs[1][:, 128:])
        inv = 1.0 / den
        inverse[:, cols] = inv
        mixed[:, cols] = (num * inv).astype(bf16)
        return carry

    lax.fori_loop(0, PAIRS, one, 0)


def use_kernel(reach, pos, sq, mixed, inverse, grad_mixed, g_out, e_out, state, total):
    cosine, sine, use, tail, keep = position_terms(pos[...], reach)

    def one(p, carry):
        cols = pl.ds(pl.multiple_of(128 * p, 128), 128)
        grad = grad_mixed[:, cols].astype(f32)
        inv = inverse[:, cols]
        g = (grad * inv).astype(bf16)
        e = -(sum_by_head(grad * mixed[:, cols].astype(f32)) * inv)
        g_out[:, cols] = g
        e_out[:, cols] = e
        soft = sq[:, cols] * use
        for k, wave in enumerate((cosine, sine)):
            feature = (soft * wave).astype(bf16)
            state[p, 64 * k : 64 * k + 64, :] = compact_of(dot(feature, g, ((0,), (0,))))
            total[k : k + 1, cols] = jnp.sum(feature.astype(f32) * e, axis=0, keepdims=True)
        total[2:3, cols] = keep
        total[3:8, cols] = jnp.zeros((5, 128), f32)
        return carry

    lax.fori_loop(0, PAIRS, one, 0)


def back_kernel(
    reach, pos, q, k, v, sq, sk, g, e, entering, entering_total, later, later_total,
    grad_q, grad_k, grad_v, mask,
):
    mask[...] = mask_of(pos[...], reach, True)
    cosine, sine, use, tail, keep = position_terms(pos[...], reach)
    side = lane_side((SUB, 128))
    lane = lax.broadcasted_iota(jnp.int32, (SUB, 128), 1)

    def sigmoid(raw):
        return 1.0 / (1.0 + jnp.exp(-raw.astype(f32)))

    def one(p, carry):
        cols = pl.ds(pl.multiple_of(128 * p, 128), 128)
        soft_q, soft_k = sq[:, cols], sk[:, cols]
        query, key = soft_q.astype(bf16), soft_k.astype(bf16)
        value, gp, ep = v[:, cols], g[:, cols], e[:, cols]
        e_high = ep.astype(bf16)
        e_low = (ep - e_high.astype(f32)).astype(bf16)
        gx = jnp.concatenate([gp, jnp.where(lane % 2 == 0, e_high, e_low)], axis=1)
        zero = jnp.zeros_like(query)
        key_t = jnp.transpose(key)
        rows_q, parts_k, parts_v = [], [], []
        for h in range(2):
            mine = side if h == 0 else jnp.logical_not(side)
            pick = jnp.where(mine, key, zero)
            probe = jnp.where((lane == 64 * h) | (lane == 64 * h + 1), 1.0, 0.0).astype(bf16)
            vx = jnp.concatenate([jnp.where(mine, value, zero), probe], axis=1)
            w_top = (dot(pick[:256], query, ((1,), (1,))) * mask[:256, :]).astype(bf16)
            w_low = (dot(pick[256:], query[256:], ((1,), (1,))) * mask[256:, 256:]).astype(bf16)
            d_top = (dot(vx[:256], gx, ((1,), (1,))) * mask[:256, :]).astype(bf16)
            d_low = (dot(vx[256:], gx[256:], ((1,), (1,))) * mask[256:, 256:]).astype(bf16)
            parts_k.append(jnp.concatenate([dot(d_top, query), dot(d_low, query[256:])], axis=0))
            parts_v.append(jnp.concatenate([dot(w_top, gp), dot(w_low, gp[256:])], axis=0))
            slim = key_t[64 * h : 64 * h + 64]
            first = dot(slim[:, :256], d_top)
            second = dot(slim[:, 256:], d_low)
            rows_q.append(jnp.concatenate([first[:, :256], first[:, 256:] + second], axis=1))
        grad_soft_q = jnp.transpose(jnp.concatenate(rows_q, axis=0))
        grad_soft_k = jnp.where(side, parts_k[0], parts_k[1])
        grad_val = jnp.where(side, parts_v[0], parts_v[1])
        wide = widen(entering[p])
        through = dot(gp, wide, ((1,), (1,)))
        grad_soft_q = grad_soft_q + use * (
            cosine * (through[:, :128] + ep * entering_total[0:1, cols])
            + sine * (through[:, 128:] + ep * entering_total[1:2, cols])
        )
        wide = widen(later[p])
        through = dot(value, wide, ((1,), (1,)))
        grad_soft_k = grad_soft_k + tail * (
            cosine * (through[:, :128] + later_total[0:1, cols])
            + sine * (through[:, 128:] + later_total[1:2, cols])
        )
        soft = soft_k * tail
        feature = jnp.concatenate([soft * cosine, soft * sine], axis=1).astype(bf16)
        grad_val = grad_val + dot(feature, wide)
        grad_q[:, cols] = (grad_soft_q * sigmoid(q[:, cols])).astype(bf16)
        grad_k[:, cols] = (grad_soft_k * sigmoid(k[:, cols])).astype(bf16)
        grad_v[:, cols] = grad_val.astype(bf16)
        return carry

    lax.fori_loop(0, PAIRS, one, 0)


def call(kernel, outs, *args, scratch=(), name=None):
    return pl.pallas_call(
        kernel,
        out_shape=tuple(jax.ShapeDtypeStruct(s, d) for s, d in outs),
        in_specs=[VMEM_SPEC] * len(args),
        out_specs=(VMEM_SPEC,) * len(outs),
        scratch_shapes=list(scratch),
        compiler_params=params(),
        name=name,
    )(*args)


def norm_rows(values, gain_factor, shift_term):
    centered = values - jnp.mean(values, axis=-1, keepdims=True)
    inv_scale = lax.rsqrt(jnp.mean(centered * centered, axis=-1, keepdims=True) + eps)
    normed = centered * inv_scale
    return (normed * gain_factor + shift_term, normed, inv_scale)


def norm_back(grad_rows, normed, inv_scale, gain_factor):
    grad_norm = grad_rows * gain_factor
    inner_term = (
        grad_norm
        - jnp.mean(grad_norm, axis=-1, keepdims=True)
        - normed * jnp.mean(grad_norm * normed, axis=-1, keepdims=True)
    )
    return (inv_scale * inner_term, jnp.sum(grad_rows * normed, axis=0), jnp.sum(grad_rows, axis=0))


def local(
    inputs, positions, w_query, w_key, w_value, w_out, w_up, bias_up, w_down, bias_down,
    gain_mid, shift_mid, gain_out, shift_out, grad_out,
):
    chips = lax.axis_size("blk")
    grid = Grid(chips)
    devices = 2 * chips
    device = lax.axis_index("head") * chips + lax.axis_index("blk")
    tokens = inputs[0]
    width = tokens.shape[1]
    reach = float(SUB * devices)
    weights = [w_query, w_key, w_value, w_out, w_up, w_down]
    small = [bias_up, bias_down, gain_mid, shift_mid, gain_out, shift_out]

    def spread(piece):
        size = piece.shape[0]
        rows = lax.broadcasted_iota(jnp.int32, (size, size * devices), 0)
        cols = lax.broadcasted_iota(jnp.int32, (size, size * devices), 1)
        spot = (cols == rows + device * size).astype(bf16)
        return dot(piece[None], spot).reshape(-1, width)

    vec = jnp.concatenate([spread(piece) for piece in small] + [jnp.zeros((7, width), f32)])
    if grid.inner > 1:
        lanes = grid.lanes()
        weights = [
            lax.all_gather(w, "blk", axis=0, tiled=True, axis_index_groups=lanes) for w in weights
        ]
        vec = lax.psum(vec, "blk", axis_index_groups=lanes)
    shapes = [w.shape for w in weights]
    (wq, wk, wv, wo, wu, wd), vec = gather_weights(grid, weights, vec)
    lift_bias, drop_bias = vec[:4].reshape(-1), vec[4]
    mid_gain, mid_shift, end_gain, end_shift = vec[5], vec[6], vec[7], vec[8]

    square, wide = (SUB, width), (PAIRS, 128, 128)
    q, k, v, sq, sk, state, total = call(
        functools.partial(projections_kernel, reach),
        [(square, bf16)] * 3 + [(square, f32)] * 2 + [(wide, f32), ((8, width), f32)],
        tokens, wq, wk, wv, positions, name="projections",
    )
    entering, entering_total = exchange_states(grid, state, total, False)
    mixed, inverse = call(
        functools.partial(attend_kernel, reach),
        [(square, bf16), (square, f32)],
        positions, sq, sk, v, entering, entering_total,
        scratch=[pltpu.VMEM((SUB, SUB), f32)], name="attend",
    )
    middle = tokens.astype(f32) + dot(mixed, wo)
    mid_rows, normed_mid, scale_mid = norm_rows(middle, mid_gain, mid_shift)
    mid_rounded = mid_rows.astype(bf16)
    up_rows = dot(mid_rounded, wu) + lift_bias
    gelu_rows, gelu_back = jax.vjp(jax.nn.gelu, up_rows)
    active = gelu_rows.astype(bf16)
    after_ffn = mid_rows + dot(active, wd) + drop_bias
    result, normed_end, scale_end = norm_rows(after_ffn, end_gain, end_shift)
    output = result.astype(bf16)[None]
    grad_rows = grad_out[0].astype(f32)
    grad_after, grad_end_gain, grad_end_shift = norm_back(
        grad_rows, normed_end, scale_end, end_gain
    )
    grad_branch = grad_after.astype(bf16)
    grad_down = dot(active, grad_branch, ((0,), (0,))).astype(bf16)
    grad_drop = jnp.sum(grad_branch, axis=0, dtype=f32)
    grad_active = dot(grad_branch, wd, ((1,), (1,)))
    grad_lift_rows = gelu_back(grad_active)[0].astype(bf16)
    grad_up = dot(mid_rounded, grad_lift_rows, ((0,), (0,))).astype(bf16)
    grad_lift = jnp.sum(grad_lift_rows, axis=0, dtype=f32)
    grad_mid_rows = dot(grad_lift_rows, wu, ((1,), (1,))) + grad_after
    grad_middle, grad_mid_gain, grad_mid_shift = norm_back(
        grad_mid_rows, normed_mid, scale_mid, mid_gain
    )
    grad_attn = grad_middle.astype(bf16)
    grad_out_weight = dot(mixed, grad_attn, ((0,), (0,))).astype(bf16)
    grad_mixed = dot(grad_attn, wo, ((1,), (1,))).astype(bf16)
    g, e, state, total = call(
        functools.partial(use_kernel, reach),
        [(square, bf16), (square, f32), (wide, f32), ((8, width), f32)],
        positions, sq, mixed, inverse, grad_mixed, name="use",
    )
    later, later_total = exchange_states(grid, state, total, True)
    grad_q, grad_k, grad_v = call(
        functools.partial(back_kernel, reach),
        [(square, bf16)] * 3,
        positions, q, k, v, sq, sk, g, e, entering, entering_total, later, later_total,
        scratch=[pltpu.VMEM((SUB, SUB), f32)], name="back",
    )
    grad_weights = [dot(tokens, r, ((0,), (0,))).astype(bf16) for r in (grad_q, grad_k, grad_v)]
    grad_inputs = grad_middle
    for r, w in ((grad_q, wq), (grad_k, wk), (grad_v, wv)):
        grad_inputs = grad_inputs + dot(r, w, ((1,), (1,)))
    vec = jnp.concatenate(
        [
            grad_lift.reshape(-1, width),
            jnp.stack([grad_drop, grad_mid_gain, grad_mid_shift, grad_end_gain, grad_end_shift]),
            jnp.zeros((7, width), f32),
        ]
    )
    summed, vec = scatter_grads(
        grid, grad_weights + [grad_out_weight, grad_up, grad_down], vec, shapes
    )
    if grid.inner > 1:
        lanes = grid.lanes()
        summed = [
            lax.psum_scatter(
                s, "blk", scatter_dimension=0, tiled=True, axis_index_groups=lanes
            )
            for s in summed
        ]
        vec = lax.psum(vec, "blk", axis_index_groups=lanes)
    pieces = []
    flat = [vec[:4].reshape(-1)] + [vec[r] for r in range(4, 9)]
    for whole, piece in zip(flat, small):
        size = piece.shape[0]
        pieces.append(lax.dynamic_slice(whole, (device * size,), (size,)))
    g_q, g_k, g_v, g_o, g_u, g_d = summed
    return (
        output, grad_inputs[None], g_q, g_k, g_v, g_o, g_u, pieces[0], g_d, *pieces[1:],
    )


def solution(mesh):
    rows = P(("head", "blk"), None)
    ones = P(("head", "blk"))
    seq = P("blk", "head", None)
    in_specs = (
        seq, P("blk", "head"), rows, rows, rows, rows, rows, ones, rows, ones, ones, ones, ones,
        ones, seq,
    )
    out_specs = (
        seq, seq, rows, rows, rows, rows, rows, ones, rows, ones, ones, ones, ones, ones,
    )
    return jax.shard_map(local, mesh=mesh, in_specs=in_specs, out_specs=out_specs, check_vma=False)
```
